32 devices in a mesh: shard: 8 (over y, x, core), rep: 4 (over z).
Axes of the slice: x: 2, y: 2, z: 4, core: 2. Of those that a mesh axis runs over, the one named last changes fastest.
Arguments:
- tokens: bfloat16 [4, 1024, 1600], P('rep', 'shard'), may hold values from -6 to 6
- segment_ids: int32 [4, 1024], P('rep'), may hold values from 0 to 3, never falling along the last dimension, each value on 1 to 512 neighbouring positions
- ln1_gain: bfloat16 [1600], P('shard'), may hold values from 0.5 to 1.5
- ln1_bias: bfloat16 [1600], P('shard'), may hold values from -2.5 to 2.5
- w_qkv: bfloat16 [1600, 4800], P('shard')
- q_bias: bfloat16 [1600], P('shard'), may hold values from -2.5 to 2.5
- v_bias: bfloat16 [1600], P('shard'), may hold values from -2.5 to 2.5
- w_out: bfloat16 [1600, 1600], P('shard'), may hold values from -0.625 to 0.625
- out_bias: bfloat16 [1600], P('shard'), may hold values from -2.5 to 2.5
- ln2_gain: bfloat16 [1600], P('shard'), may hold values from 0.5 to 1.5
- ln2_bias: bfloat16 [1600], P('shard'), may hold values from -2.5 to 2.5
- w_fc: bfloat16 [1600, 6400], P('shard'), may hold values from -0.15625 to 0.15625
- fc_bias: bfloat16 [6400], P('shard'), may hold values from -2.5 to 2.5
- w_proj: bfloat16 [6400, 1600], P('shard'), may hold values from -0.078125 to 0.078125
- proj_bias: bfloat16 [1600], P('shard'), may hold values from -2.5 to 2.5
- grad_out: bfloat16 [4, 1024, 1600], P('rep', 'shard'), may hold values from -6 to 6
Outputs:
- output: float32 [4, 1024, 1600], P('rep', 'shard')
- grad_tokens: float32 [4, 1024, 1600], P('rep', 'shard')
- grad_ln1_gain: float32 [1600], P('shard')
- grad_ln1_bias: float32 [1600], P('shard')
- grad_w_qkv: float32 [1600, 4800], P('shard', 'rep')
- grad_q_bias: float32 [1600], P('shard')
- grad_v_bias: float32 [1600], P('shard')
- grad_w_out: float32 [1600, 1600], P('shard', 'rep')
- grad_out_bias: float32 [1600], P('shard')
- grad_ln2_gain: float32 [1600], P('shard')
- grad_ln2_bias: float32 [1600], P('shard')
- grad_w_fc: float32 [1600, 6400], P('shard', 'rep')
- grad_fc_bias: float32 [6400], P('shard')
- grad_w_proj: float32 [6400, 1600], P('shard', 'rep')
- grad_proj_bias: float32 [1600], P('shard')
The draws below stay inside these ranges and needn't reach their ends.
Inputs may be any that keep to these rules, and one draw needn't show every extreme that they name: `segment_ids`: along each sequence the document numbers never fall, and one document covers at most 512 positions.
All inputs are finite; a program needn't handle non-finite values.
Results may differ from the reference program's by a relative error of at most 0.019.
Values may be sent and summed in bfloat16 or wider, within the bound.
No kernel may reach another device: no remote copies, remote signals or barrier semaphores. Data moves between devices by JAX's collectives and lax.ppermute only.
A program may use at most 576 MiB of HBM per device.

```python
import math
import jax
import jax.numpy as jnp
import numpy as np
from jax import lax

HD = 64
D = 1600
FF = 6400
L = 1024
SEGS = 4
B = 4


def draw_w_qkv(key, part):
    key_base = jax.random.fold_in(key, 11)
    base = jax.random.normal(key_base, (D, 3 * D), jnp.float32) * float(D) ** (-0.5)
    return base.astype(jnp.bfloat16)


def steps_of(stream_key, dims, cuts, smallest, top_value):
    loudness = 1.0
    for dim, blocks in cuts:
        heights = jax.random.uniform(jax.random.fold_in(jax.random.fold_in(stream_key, 6), dim), (blocks,), jnp.float32, smallest / len(cuts), top_value / len(cuts))
        loudness = loudness * jnp.repeat(jnp.exp(heights), dims[dim] // blocks).reshape((-1,) + (1,) * (len(dims) - 1 - dim))
    return loudness


def split_up(count, total, most, skew):
    portions = [(1 << 20) // math.isqrt(standing ** skew) + 1 for standing in range(2, count + 1)]
    rest, given = total - most - (count - 1), [1] * (count - 1)
    while rest > 0:
        movable = [i for i in range(count - 1) if given[i] < most]
        whole, left = sum([portions[i] for i in movable]), rest
        for i in movable:
            extra = min(most - given[i], max(1, left * portions[i] // whole), rest)
            given[i] = given[i] + extra
            rest = rest - extra
    return np.array([most] + given)


def ragged_sizes(own_key, number_of, total, reach, skew):
    if number_of == 2:
        one = jax.random.randint(own_key, (), max(1, total - reach), min(reach, total - 1) + 1)
        return jnp.stack([one, total - one])
    tallies = jnp.asarray(split_up(number_of, total, reach, skew), jnp.int32)
    twos = (number_of - 1) // 2
    donor, sink = tallies[1:1 + 2 * twos:2], tallies[2:2 + 2 * twos:2]
    margin = jnp.minimum(donor - 1, reach - sink)
    moved = jax.random.randint(jax.random.fold_in(own_key, 1), (twos,), 0, 1 << 20) % (margin + 1)
    tallies = tallies.at[1:1 + 2 * twos:2].set(donor - moved).at[2:2 + 2 * twos:2].set(sink + moved)
    return tallies[jax.random.permutation(jax.random.fold_in(own_key, 2), number_of)]


def scatter_about(rng, shape, scale, limit, split=(), kind=jnp.bfloat16):
    loudness = steps_of(rng, shape, split, -0.22, 0.18) if split else 1.0
    array = jax.random.normal(rng, shape, jnp.float32) * scale * loudness
    return jnp.minimum(jnp.maximum(array, -limit), limit).astype(kind)


def setup_inputs(seed: int = 0) -> dict:
    seeds = jax.random.split(jax.random.key(seed), 17)
    tokens = scatter_about(seeds[0], (B, L, D), 1.0, 6.0, ((0, 4), (1, 8)))
    segment_ids = jax.vmap(lambda own: jnp.searchsorted(jnp.cumsum(ragged_sizes(own, SEGS, L, L // 2, 2)), jnp.arange(L), side="right"))(jax.random.split(seeds[1], B)).reshape((B, L)).astype(jnp.int32)
    ln1_gain = jnp.clip(1.0 + 0.1 * jax.random.normal(seeds[2], (D,), jnp.float32), 0.5, 1.5).astype(jnp.bfloat16)
    ln1_bias = scatter_about(seeds[3], (D,), 0.3, 2.5, ((0, 8),))
    w_qkv = draw_w_qkv(jax.random.fold_in(seeds[16], 71), 0)
    q_bias = scatter_about(seeds[5], (D,), 0.3, 2.5, ((0, 8),))
    v_bias = scatter_about(seeds[6], (D,), 0.3, 2.5, ((0, 8),))
    w_out = scatter_about(seeds[7], (D, D), (D // 16) ** -0.5, 0.625, ((0, 8),))
    out_bias = scatter_about(seeds[8], (D,), 0.3, 2.5, ((0, 8),))
    ln2_gain = jnp.clip(1.0 + 0.1 * jax.random.normal(seeds[9], (D,), jnp.float32), 0.5, 1.5).astype(jnp.bfloat16)
    ln2_bias = scatter_about(seeds[10], (D,), 0.3, 2.5, ((0, 8),))
    w_fc = scatter_about(seeds[11], (D, FF), D ** -0.5, 0.15625, ((0, 8),))
    fc_bias = scatter_about(seeds[12], (FF,), 0.3, 2.5, ((0, 8),))
    w_proj = scatter_about(seeds[13], (FF, D), FF ** -0.5, 0.078125, ((0, 8),))
    proj_bias = scatter_about(seeds[14], (D,), 0.3, 2.5, ((0, 8),))
    grad_out = scatter_about(seeds[15], (B, L, D), 1.0, 6.0, ((0, 4), (1, 8)))
    return dict(tokens=tokens, segment_ids=segment_ids, ln1_gain=ln1_gain, ln1_bias=ln1_bias, w_qkv=w_qkv, q_bias=q_bias, v_bias=v_bias, w_out=w_out, out_bias=out_bias, ln2_gain=ln2_gain, ln2_bias=ln2_bias, w_fc=w_fc, fc_bias=fc_bias, w_proj=w_proj, proj_bias=proj_bias, grad_out=grad_out)


EPSILON = 1e-05
GELU_SCALE = math.sqrt(2.0 / math.pi)

def rounded(values):
    return lax.optimization_barrier(values.astype(jnp.bfloat16)).astype(jnp.float32)

def layer_norm(values, gain, shift):
    centre_val = lax.optimization_barrier(jnp.mean(values, axis=-1, keepdims=True))
    centred = values - centre_val
    variance = lax.optimization_barrier(jnp.mean(centred * centred, axis=-1, keepdims=True))
    inverse = lax.rsqrt(variance + EPSILON)
    normed = centred * inverse
    return (normed * gain + shift, normed, inverse)

def norm_back(upstream, normed, inverse, gain):
    scaled = upstream * gain
    return inverse * (scaled - lax.optimization_barrier(jnp.mean(scaled, axis=-1, keepdims=True)) - normed * lax.optimization_barrier(jnp.mean(scaled * normed, axis=-1, keepdims=True)))

def gelu_value(inputs_pre):
    cubic = inputs_pre * inputs_pre * inputs_pre
    return 0.5 * inputs_pre * (1.0 + jnp.tanh(GELU_SCALE * (inputs_pre + 0.044715 * cubic)))

def gelu_slope(inputs_pre):
    square = inputs_pre * inputs_pre
    tangent = jnp.tanh(GELU_SCALE * (inputs_pre + 0.044715 * square * inputs_pre))
    return 0.5 * (1.0 + tangent) + 0.5 * inputs_pre * (1.0 - tangent * tangent) * GELU_SCALE * (1.0 + 3.0 * 0.044715 * square)

def score_table(queries, keys, key_mask, score_scale):
    scores = jnp.einsum('sqhe,skhe->shqk', queries.astype(jnp.float32), keys.astype(jnp.float32)) * score_scale
    return jnp.where(key_mask[:, None], scores, -1e+30)

def attend(queries, keys, values, key_mask, score_scale):
    scores = score_table(queries, keys, key_mask, score_scale)
    row_max = lax.optimization_barrier(jnp.max(scores, axis=-1, keepdims=True))
    log_total = row_max + jnp.log(lax.optimization_barrier(jnp.sum(jnp.exp(scores - row_max), axis=-1, keepdims=True)))
    weights_soft = jnp.where(key_mask[:, None], jnp.exp(scores - log_total), 0.0)
    mixed = jnp.einsum('shqk,skhe->sqhe', rounded(weights_soft), values.astype(jnp.float32))
    return (mixed, log_total)

def attend_back(queries, keys, values, key_mask, log_total, grad_mixed, score_scale):
    scores = score_table(queries, keys, key_mask, score_scale)
    weights_soft = jnp.where(key_mask[:, None], jnp.exp(scores - log_total), 0.0)
    grad_soft = jnp.einsum('sqhe,skhe->shqk', grad_mixed.astype(jnp.float32), values.astype(jnp.float32))
    delta = lax.optimization_barrier(jnp.sum(weights_soft * grad_soft, axis=-1, keepdims=True))
    grad_scores = rounded(weights_soft * (grad_soft - delta) * score_scale)
    grad_q = jnp.einsum('shqk,skhe->sqhe', grad_scores, keys.astype(jnp.float32))
    grad_k = jnp.einsum('shqk,sqhe->skhe', grad_scores, queries.astype(jnp.float32))
    grad_v = jnp.einsum('shqk,sqhe->skhe', rounded(weights_soft), grad_mixed.astype(jnp.float32))
    return (grad_q, grad_k, grad_v)

def reference(tokens, segment_ids, ln1_gain, ln1_bias, w_qkv, q_bias, v_bias, w_out, out_bias, ln2_gain, ln2_bias, w_fc, fc_bias, w_proj, proj_bias, grad_out):
    head_count = D // HD
    score_scale = float(HD) ** (-0.5)
    gain_one = ln1_gain.astype(jnp.float32)
    shift_one = ln1_bias.astype(jnp.float32)
    bias_q = q_bias.astype(jnp.float32)
    bias_v = v_bias.astype(jnp.float32)
    bias_out = out_bias.astype(jnp.float32)
    gain_two = ln2_gain.astype(jnp.float32)
    shift_two = ln2_bias.astype(jnp.float32)
    bias_fc = fc_bias.astype(jnp.float32)
    bias_proj = proj_bias.astype(jnp.float32)
    position = jnp.arange(L, dtype=jnp.int32)
    causal = position[None, :] <= position[:, None]

    def one_sequence(carry, items):
        token_seq, seg_seq, grad_seq = items
        resid_in = token_seq.astype(jnp.float32)
        ln_one, normed_one, inverse_one = layer_norm(resid_in, gain_one, shift_one)
        ln_one_b = ln_one.astype(jnp.bfloat16)
        qkv = jnp.dot(ln_one_b, w_qkv, preferred_element_type=jnp.float32)
        queries = (qkv[:, :D] + bias_q).astype(jnp.bfloat16).reshape(1, L, head_count, HD)
        keys = qkv[:, D:2 * D].astype(jnp.bfloat16).reshape(1, L, head_count, HD)
        values = (qkv[:, 2 * D:] + bias_v).astype(jnp.bfloat16).reshape(1, L, head_count, HD)
        key_mask = (causal & (seg_seq[None, :] == seg_seq[:, None]))[None]
        mixed, log_total = attend(queries, keys, values, key_mask, score_scale)
        attended = mixed.reshape(L, D).astype(jnp.bfloat16)
        mid = resid_in + jnp.dot(attended, w_out, preferred_element_type=jnp.float32) + bias_out
        ln_two, normed_two, inverse_two = layer_norm(mid, gain_two, shift_two)
        ln_two_b = ln_two.astype(jnp.bfloat16)
        pre_act = jnp.dot(ln_two_b, w_fc, preferred_element_type=jnp.float32) + bias_fc
        hidden = gelu_value(pre_act).astype(jnp.bfloat16)
        result = mid + jnp.dot(hidden, w_proj, preferred_element_type=jnp.float32) + bias_proj
        grad_top = grad_seq.astype(jnp.float32)
        g_proj = jnp.dot(hidden.T, grad_seq, preferred_element_type=jnp.float32)
        grad_hidden = jnp.dot(grad_seq, w_proj.T, preferred_element_type=jnp.float32)
        grad_pre = grad_hidden * gelu_slope(pre_act)
        grad_pre_round = grad_pre.astype(jnp.bfloat16)
        g_fc = jnp.dot(ln_two_b.T, grad_pre_round, preferred_element_type=jnp.float32)
        grad_ln_two = jnp.dot(grad_pre_round, w_fc.T, preferred_element_type=jnp.float32)
        grad_mid = grad_top + norm_back(grad_ln_two, normed_two, inverse_two, gain_two)
        grad_mid_round = grad_mid.astype(jnp.bfloat16)
        g_out = jnp.dot(attended.T, grad_mid_round, preferred_element_type=jnp.float32)
        grad_attended = jnp.dot(grad_mid_round, w_out.T, preferred_element_type=jnp.float32).astype(jnp.bfloat16)
        grad_q, grad_k, grad_v = attend_back(queries, keys, values, key_mask, log_total, grad_attended.reshape(1, L, head_count, HD), score_scale)
        grad_q = grad_q.reshape(L, D)
        grad_k = grad_k.reshape(L, D)
        grad_v = grad_v.reshape(L, D)
        grad_qkv = jnp.concatenate([grad_q, grad_k, grad_v], axis=1).astype(jnp.bfloat16)
        g_qkv = jnp.dot(ln_one_b.T, grad_qkv, preferred_element_type=jnp.float32)
        grad_ln_one = jnp.dot(grad_qkv, w_qkv.T, preferred_element_type=jnp.float32)
        grad_in = grad_mid + norm_back(grad_ln_one, normed_one, inverse_one, gain_one)
        terms = (lax.optimization_barrier(jnp.sum(grad_ln_one * normed_one, axis=0)), lax.optimization_barrier(jnp.sum(grad_ln_one, axis=0)), g_qkv, lax.optimization_barrier(jnp.sum(grad_q, axis=0)), lax.optimization_barrier(jnp.sum(grad_v, axis=0)), g_out, lax.optimization_barrier(jnp.sum(grad_mid, axis=0)), lax.optimization_barrier(jnp.sum(grad_ln_two * normed_two, axis=0)), lax.optimization_barrier(jnp.sum(grad_ln_two, axis=0)), g_fc, lax.optimization_barrier(jnp.sum(grad_pre, axis=0)), g_proj, lax.optimization_barrier(jnp.sum(grad_top, axis=0)))
        summed = tuple((before + term for before, term in zip(carry, terms)))
        return (summed, (result, grad_in))
    start_carry = (jnp.zeros((D,), jnp.float32), jnp.zeros((D,), jnp.float32), jnp.zeros((D, 3 * D), jnp.float32), jnp.zeros((D,), jnp.float32), jnp.zeros((D,), jnp.float32), jnp.zeros((D, D), jnp.float32), jnp.zeros((D,), jnp.float32), jnp.zeros((D,), jnp.float32), jnp.zeros((D,), jnp.float32), jnp.zeros((D, FF), jnp.float32), jnp.zeros((FF,), jnp.float32), jnp.zeros((FF, D), jnp.float32), jnp.zeros((D,), jnp.float32))
    grads, (output, grad_tokens) = lax.scan(one_sequence, start_carry, (tokens, segment_ids, grad_out))
    return (output, grad_tokens, grads[0], grads[1], grads[2], grads[3], grads[4], grads[5], grads[6], grads[7], grads[8], grads[9], grads[10], grads[11], grads[12])
```

```python
import functools
import math

import jax
import jax.numpy as jnp
from jax import lax
from jax.experimental import pallas as pl
from jax.experimental.pallas import tpu as pltpu
from jax.sharding import PartitionSpec as P

HD = 64
MAX_DOC = 512

EPSILON = 1e-05
GELU_SCALE = math.sqrt(2.0 / math.pi)
BF16 = jnp.bfloat16
F32 = jnp.float32
NEG = -1e30
PAIR = 2 * HD


def layer_norm(values, gain, shift):
    centre_val = jnp.mean(values, axis=-1, keepdims=True)
    centred = values - centre_val
    variance = jnp.mean(centred * centred, axis=-1, keepdims=True)
    inverse = lax.rsqrt(variance + EPSILON)
    normed = centred * inverse
    return (normed * gain + shift, normed, inverse)


def norm_back(upstream, normed, inverse, gain):
    scaled = upstream * gain
    return inverse * (
        scaled
        - jnp.mean(scaled, axis=-1, keepdims=True)
        - normed * jnp.mean(scaled * normed, axis=-1, keepdims=True)
    )


def gelu_both(inputs_pre):
    square = inputs_pre * inputs_pre
    tangent = jnp.tanh(GELU_SCALE * (inputs_pre + 0.044715 * square * inputs_pre))
    value = 0.5 * inputs_pre * (1.0 + tangent)
    slope = 0.5 * (1.0 + tangent) + 0.5 * inputs_pre * (1.0 - tangent * tangent) * GELU_SCALE * (
        1.0 + 3.0 * 0.044715 * square
    )
    return value, slope


def dot_nn(a, b):
    return lax.dot_general(a, b, (((1,), (0,)), ((), ())), preferred_element_type=F32)


def dot_nt(a, b):
    return lax.dot_general(a, b, (((1,), (1,)), ((), ())), preferred_element_type=F32)


def dot_tn(a, b):
    return lax.dot_general(a, b, (((0,), (0,)), ((), ())), preferred_element_type=F32)


def block_at(me, j, count):
    k = jnp.bitwise_xor(me, j)
    return jnp.bitwise_and(k, 1) * (count // 2) + jnp.right_shift(k, 1)


def window_of(i, rows):
    back = -(-MAX_DOC // rows)
    return max(0, i - back) * rows, (i + 1) * rows


def mask_of(seg_row, seg_col, i, rows):
    lo, hi = window_of(i, rows)
    first = i * rows
    query_pos = first + lax.broadcasted_iota(jnp.int32, (rows, hi - lo), 0)
    key_pos = lo + lax.broadcasted_iota(jnp.int32, (rows, hi - lo), 1)
    same = seg_col[first : first + rows, :] == seg_row[:, lo:hi]
    return (key_pos <= query_pos) & same


def fwd_kernel(scale, rows, me_ref, seg_row, seg_col, qkv_ref, out_ref, lse_ref, ks, vs):
    count, part, width = qkv_ref.shape
    third = width // 3
    me = me_ref[0]
    spots = [block_at(me, j, count) for j in range(count)]
    per = rows // part
    left = lax.broadcasted_iota(jnp.int32, (1, PAIR), 1) < HD
    for pair in range(third // PAIR):
        at = pair * PAIR
        for j in range(count):
            ks[j * part : (j + 1) * part, :] = qkv_ref[spots[j], :, third + at : third + at + PAIR]
            vs[j * part : (j + 1) * part, :] = qkv_ref[
                spots[j], :, 2 * third + at : 2 * third + at + PAIR
            ]
        for i in range(count // per):
            lo, hi = window_of(i, rows)
            mask = mask_of(seg_row, seg_col, i, rows)
            q = jnp.concatenate(
                [qkv_ref[spots[i * per + b], :, at : at + PAIR] for b in range(per)], axis=0
            )
            kk, vv = ks[lo:hi, :], vs[lo:hi, :]
            mixed, totals = [], []
            for side in (left, ~left):
                qm = jnp.where(side, q, jnp.zeros_like(q))
                s = jnp.where(mask, dot_nt(qm, kk) * scale, NEG)
                top = jnp.max(s, axis=-1, keepdims=True)
                e = jnp.exp(s - top)
                total = jnp.sum(e, axis=-1, keepdims=True)
                mixed.append(dot_nn((e * (1.0 / total)).astype(BF16), vv))
                totals.append(top + jnp.log(total))
            o = jnp.where(left, mixed[0], mixed[1]).astype(BF16)
            t = jnp.where(left, totals[0], totals[1])
            for b in range(per):
                out_ref[spots[i * per + b], :, at : at + PAIR] = o[b * part : (b + 1) * part, :]
                lse_ref[spots[i * per + b], :, at : at + PAIR] = t[b * part : (b + 1) * part, :]


def bwd_kernel(
    scale, rows, me_ref, seg_row, seg_col, qkv_ref, grad_ref, lse_ref, out_ref, sum_ref, ks, vs, dk, dv
):
    count, part, width = qkv_ref.shape
    third = width // 3
    me = me_ref[0]
    spots = [block_at(me, j, count) for j in range(count)]
    per = rows // part
    left = lax.broadcasted_iota(jnp.int32, (1, PAIR), 1) < HD
    sum_ref[...] = jnp.zeros_like(sum_ref)
    for pair in range(third // PAIR):
        at = pair * PAIR
        for j in range(count):
            ks[j * part : (j + 1) * part, :] = qkv_ref[spots[j], :, third + at : third + at + PAIR]
            vs[j * part : (j + 1) * part, :] = qkv_ref[
                spots[j], :, 2 * third + at : 2 * third + at + PAIR
            ]
        dk[...] = jnp.zeros_like(dk)
        dv[...] = jnp.zeros_like(dv)
        q_sum = jnp.zeros((1, PAIR), F32)
        for i in range(count // per):
            lo, hi = window_of(i, rows)
            mask = mask_of(seg_row, seg_col, i, rows)
            here = [spots[i * per + b] for b in range(per)]
            q = jnp.concatenate([qkv_ref[h, :, at : at + PAIR] for h in here], axis=0)
            g = jnp.concatenate([grad_ref[h, :, at : at + PAIR] for h in here], axis=0)
            t = jnp.concatenate([lse_ref[h, :, at : at + PAIR] for h in here], axis=0)
            kk, vv = ks[lo:hi, :], vs[lo:hi, :]
            dq = None
            for number, side in enumerate((left, ~left)):
                qm = jnp.where(side, q, jnp.zeros_like(q))
                gm = jnp.where(side, g, jnp.zeros_like(g))
                km = jnp.where(side, kk, jnp.zeros_like(kk))
                lse = t[:, number * HD : number * HD + 1]
                probs = jnp.where(mask, jnp.exp(dot_nt(qm, kk) * scale - lse), 0.0)
                dp = dot_nt(gm, vv)
                delta = jnp.sum(probs * dp, axis=-1, keepdims=True)
                ds = (probs * (dp - delta) * scale).astype(BF16)
                part_q = dot_nn(ds, km)
                dq = part_q if dq is None else dq + part_q
                dk[lo:hi, :] += dot_tn(ds, qm)
                dv[lo:hi, :] += dot_tn(probs.astype(BF16), gm)
            q_sum = q_sum + jnp.sum(dq, axis=0, keepdims=True)
            dq = dq.astype(BF16)
            for b in range(per):
                out_ref[here[b], :, at : at + PAIR] = dq[b * part : (b + 1) * part, :]
        sum_ref[0:1, at : at + PAIR] = q_sum
        sum_ref[0:1, 2 * third + at : 2 * third + at + PAIR] = jnp.sum(
            dv[...], axis=0, keepdims=True
        )
        for j in range(count):
            out_ref[spots[j], :, third + at : third + at + PAIR] = dk[
                j * part : (j + 1) * part, :
            ].astype(BF16)
            out_ref[spots[j], :, 2 * third + at : 2 * third + at + PAIR] = dv[
                j * part : (j + 1) * part, :
            ].astype(BF16)


def attention_calls(count, part, slots, scale):
    length = count * part
    rows = 2 * part
    third = slots * HD
    vm = pl.BlockSpec(memory_space=pltpu.VMEM)
    sm = pl.BlockSpec(memory_space=pltpu.SMEM)
    fwd = pl.pallas_call(
        functools.partial(fwd_kernel, scale, rows),
        out_shape=(
            jax.ShapeDtypeStruct((count, part, third), BF16),
            jax.ShapeDtypeStruct((count, part, third), F32),
        ),
        in_specs=[sm, vm, vm, vm],
        out_specs=(vm, vm),
        scratch_shapes=[pltpu.VMEM((length, PAIR), BF16)] * 2,
        cost_estimate=pl.CostEstimate(
            flops=4 * length * length * third,
            bytes_accessed=length * third * 14,
            transcendentals=length * length * slots,
        ),
    )
    bwd = pl.pallas_call(
        functools.partial(bwd_kernel, scale, rows),
        out_shape=(
            jax.ShapeDtypeStruct((count, part, 3 * third), BF16),
            jax.ShapeDtypeStruct((8, 3 * third), F32),
        ),
        in_specs=[sm, vm, vm, vm, vm, vm],
        out_specs=(vm, vm),
        scratch_shapes=[pltpu.VMEM((length, PAIR), BF16)] * 2
        + [pltpu.VMEM((length, PAIR), F32)] * 2,
        cost_estimate=pl.CostEstimate(
            flops=10 * length * length * third,
            bytes_accessed=length * third * 18,
            transcendentals=length * length * slots,
        ),
    )
    return fwd, bwd


def exchange(x, k):
    n = lax.axis_size("shard")
    return lax.ppermute(x, "shard", [(i, i ^ k) for i in range(n)])


def gather_halves(x):
    n = lax.axis_size("shard")
    near = jnp.concatenate([x] + [exchange(x, k) for k in range(2, n, 2)], axis=0)
    return near, exchange(near, 1)


def scatter_halves(far, near):
    n = lax.axis_size("shard")
    rows = near.shape[0] // (n // 2)
    total = near + exchange(far, 1).astype(F32)
    out = total[:rows]
    for i, k in enumerate(range(2, n, 2)):
        send = total[(i + 1) * rows : (i + 2) * rows].astype(BF16)
        out = out + exchange(send, k).astype(F32)
    return out


def swap_blocks(blocks):
    n = lax.axis_size("shard")
    me = lax.axis_index("shard")
    out = blocks
    for k in range(1, n):
        there = jnp.bitwise_xor(me, k)
        got = exchange(lax.dynamic_index_in_dim(blocks, there, 0, keepdims=False), k)
        out = lax.dynamic_update_index_in_dim(out, got, there, 0)
    return out


def sum_all(x):
    for axis in ("shard", "rep"):
        size = lax.axis_size(axis)
        k = 1
        while k < size:
            x = x + lax.ppermute(x, axis, [(i, i ^ k) for i in range(size)])
            k *= 2
    return x


def after(value, *others):
    return lax.optimization_barrier((value,) + others)[0]


def local(
    tokens,
    segment_ids,
    ln1_gain,
    ln1_bias,
    w_qkv,
    q_bias,
    v_bias,
    w_out,
    out_bias,
    ln2_gain,
    ln2_bias,
    w_fc,
    fc_bias,
    w_proj,
    proj_bias,
    grad_out,
):
    seq_count, part, width = tokens.shape
    length = segment_ids.shape[1]
    n = lax.axis_size("shard")
    n_rep = lax.axis_size("rep")
    me = lax.axis_index("shard")
    own = ln1_gain.shape[0]
    own_hidden = fc_bias.shape[0]
    hidden_width = w_fc.shape[1]
    heads = width // HD
    scale = float(HD) ** (-0.5)

    first_head = [-(-own * d // HD) for d in range(n + 1)]
    n_heads = [first_head[d + 1] - first_head[d] for d in range(n)]
    slots = 2 * -(-max(n_heads) // 2)
    third = slots * HD
    spill = max(HD * first_head[d] - own * d for d in range(n))
    head_at = jnp.array([HD * h for h in first_head[:n]], jnp.int32)[me]
    head_shift = head_at - own * me
    head_rows = HD * jnp.array(n_heads, jnp.int32)[me]

    x_own = tokens.reshape(part, width)
    x_near, x_far = gather_halves(x_own)
    vectors = (ln1_gain, ln1_bias, q_bias, v_bias, out_bias, ln2_gain, ln2_bias, proj_bias)
    lanes = 128 * -(-own // 128)
    packed = jnp.pad(jnp.stack(vectors), ((0, 0), (0, lanes - own)))
    everyone = jnp.take(
        jnp.concatenate(gather_halves(packed[None]), axis=0),
        block_at(me, jnp.arange(n, dtype=jnp.int32), n),
        axis=0,
    )
    gain_one, shift_one, bias_q, bias_v, bias_out, gain_two, shift_two, bias_proj = [
        everyone[:, i, :own].reshape(width).astype(F32) for i in range(len(vectors))
    ]
    pieces = []
    for d in range(n):
        cols = []
        for c in range(3):
            lo = c * width + HD * first_head[d]
            hi = lo + HD * n_heads[d]
            cols.append(jnp.pad(w_qkv[:, lo:hi], ((0, 0), (0, third - (hi - lo)))))
        pieces.append(jnp.concatenate(cols, axis=1))
    qkv_w = swap_blocks(jnp.stack(pieces)).reshape(width, 3 * third)

    live = jnp.arange(third) < head_rows
    own_heads = lambda v: jnp.where(
        live, lax.dynamic_slice_in_dim(jnp.pad(v, (0, third)), head_at, third, 0), 0.0
    )
    bias_heads = jnp.concatenate([own_heads(bias_q), jnp.zeros(third, F32), own_heads(bias_v)])

    def first_half(x):
        ln_b = layer_norm(x.astype(F32), gain_one, shift_one)[0].astype(BF16)
        return ln_b, (dot_nn(ln_b, qkv_w) + bias_heads).astype(BF16)

    ln_one_near, qkv_near = first_half(x_near)
    ln_one_far, qkv_far = first_half(x_far)
    qkv = jnp.concatenate([qkv_near, qkv_far], axis=0).reshape(n, part, 3 * third)

    w_fc_sent = jnp.stack([w_fc[:, d * own_hidden : (d + 1) * own_hidden] for d in range(n)])
    fc_w = swap_blocks(after(w_fc_sent, qkv)).reshape(width, own_hidden)
    g_own = grad_out.reshape(part, width)
    g_near, g_far = gather_halves(after(g_own, qkv))
    out_next = lax.ppermute(w_out[:spill], "shard", [(i, i - 1) for i in range(1, n)])
    out_ext = jnp.concatenate([w_out, out_next, jnp.zeros((third, width), BF16)], axis=0)
    out_w = jnp.where(
        live[:, None], lax.dynamic_slice_in_dim(out_ext, head_shift, third, 0), 0.0
    ).astype(BF16)

    seg_row = segment_ids.reshape(1, length)
    seg_col = segment_ids.reshape(length, 1)
    me_word = me.astype(jnp.int32).reshape(1)
    attend, attend_back = attention_calls(n, part, slots, scale)
    attended, lse = attend(me_word, seg_row, seg_col, qkv)
    attended = attended.reshape(length, third)
    half = length // 2
    attn_own = scatter_halves(
        dot_nn(attended[half:], out_w).astype(BF16), dot_nn(attended[:half], out_w)
    )
    resid_in = x_own.astype(F32)
    mid = resid_in + attn_own + bias_out

    ln_two, normed_two, inverse_two = layer_norm(mid, gain_two, shift_two)
    ln_two_near, ln_two_far = gather_halves(ln_two.astype(BF16))
    bias_fc = fc_bias.astype(F32)

    def middle(ln_b, g):
        pre = dot_nn(ln_b, fc_w) + bias_fc
        value, slope = gelu_both(pre)
        grad_pre = dot_nt(g, w_proj) * slope
        return value.astype(BF16), grad_pre.astype(BF16), jnp.sum(grad_pre, axis=0)

    hidden_near, grad_pre_near, sum_near = middle(ln_two_near, g_near)
    hidden_far, grad_pre_far, sum_far = middle(ln_two_far, g_far)
    grad_ln_two = scatter_halves(
        dot_nt(grad_pre_far, fc_w).astype(BF16), dot_nt(grad_pre_near, fc_w)
    )
    hidden = jnp.concatenate([hidden_near, hidden_far], axis=0)
    g_all = jnp.concatenate([g_near, g_far], axis=0)
    grad_pre_all = jnp.concatenate([grad_pre_near, grad_pre_far], axis=0)
    ln_two_all = jnp.concatenate([ln_two_near, ln_two_far], axis=0)
    part_proj = dot_tn(hidden, g_all).astype(BF16)
    total_proj = lax.psum_scatter(
        part_proj.reshape(own_hidden, n_rep, width // n_rep).transpose(1, 0, 2),
        "rep",
        scatter_dimension=0,
    ).astype(F32)
    result = mid + bias_proj + scatter_halves(
        dot_nn(hidden_far, w_proj).astype(BF16), dot_nn(hidden_near, w_proj)
    )
    part_fc = dot_tn(ln_two_all, grad_pre_all).astype(BF16).reshape(n, own, own_hidden)
    swapped_fc = swap_blocks(part_fc)
    if n_rep <= n:
        swapped_fc = swapped_fc.reshape(n_rep, n // n_rep, own, own_hidden)
        total_fc = lax.psum_scatter(swapped_fc, "rep", scatter_dimension=0)
        total_fc = total_fc.transpose(1, 0, 2).reshape(own, hidden_width // n_rep).astype(F32)
    else:
        swapped_fc = swapped_fc.reshape(n, own, n_rep // n, hidden_width // n_rep)
        swapped_fc = swapped_fc.transpose(0, 2, 1, 3).reshape(n_rep, own, hidden_width // n_rep)
        total_fc = lax.psum_scatter(swapped_fc, "rep", scatter_dimension=0).astype(F32)

    grad_top = g_own.astype(F32)
    grad_mid = grad_top + norm_back(grad_ln_two, normed_two, inverse_two, gain_two)

    gm_near, gm_far = gather_halves(grad_mid.astype(BF16))
    grad_att = jnp.concatenate(
        [dot_nt(gm_near, out_w).astype(BF16), dot_nt(gm_far, out_w).astype(BF16)], axis=0
    ).reshape(n, part, third)
    grad_qkv, head_sums = attend_back(me_word, seg_row, seg_col, qkv, grad_att, lse)
    grad_qkv = grad_qkv.reshape(length, 3 * third)
    ln_one_all = jnp.concatenate([ln_one_near, ln_one_far], axis=0)
    part_qkv = dot_tn(ln_one_all, grad_qkv).astype(BF16).reshape(n, own, 3 * third)
    swapped_qkv = swap_blocks(part_qkv)
    whole_qkv = jnp.concatenate(
        [
            swapped_qkv[d, :, c * third : c * third + HD * n_heads[d]]
            for c in range(3)
            for d in range(n)
        ],
        axis=1,
    )
    total_qkv = lax.psum_scatter(
        whole_qkv.reshape(own, n_rep, 3 * width // n_rep).transpose(1, 0, 2),
        "rep",
        scatter_dimension=0,
    ).astype(F32)
    grad_ln_one = scatter_halves(
        dot_nt(grad_qkv[half:], qkv_w).astype(BF16), dot_nt(grad_qkv[:half], qkv_w)
    )

    gm_all = jnp.concatenate([gm_near, gm_far], axis=0)
    part_out = dot_tn(attended, gm_all).astype(BF16)
    head_out = lax.psum_scatter(
        part_out.reshape(third, n_rep, width // n_rep).transpose(1, 0, 2),
        "rep",
        scatter_dimension=0,
    )
    shifted = lax.dynamic_update_slice_in_dim(
        jnp.zeros((own + spill + third, width // n_rep), BF16), head_out, head_shift, 0
    )
    before = lax.ppermute(
        shifted[own : own + spill], "shard", [(i, i + 1) for i in range(n - 1)]
    )
    total_out = shifted[:own].astype(F32) + jnp.pad(
        before.astype(F32), ((0, own - spill), (0, 0))
    )

    _, normed_one, inverse_one = layer_norm(resid_in, gain_one, shift_one)
    grad_in = grad_mid + norm_back(grad_ln_one, normed_one, inverse_one, gain_one)

    def spread(v, start, total):
        room = jnp.zeros(total + v.shape[0], F32)
        return lax.dynamic_update_slice_in_dim(room, v, start, 0)[:total]

    spread_heads = lambda v: spread(jnp.where(live, v, 0.0), head_at, width)
    sums = [
        jnp.sum(grad_ln_one * normed_one, axis=0),
        jnp.sum(grad_ln_one, axis=0),
        spread_heads(head_sums[0, :third]),
        spread_heads(head_sums[0, 2 * third :]),
        jnp.sum(grad_mid, axis=0),
        jnp.sum(grad_ln_two * normed_two, axis=0),
        jnp.sum(grad_ln_two, axis=0),
        jnp.sum(grad_top, axis=0),
    ]
    hidden_sum = spread(sum_near + sum_far, own_hidden * me, hidden_width)
    flat = jnp.concatenate(sums + [hidden_sum]).reshape(-1, width)
    flat = sum_all(flat)
    mine = lax.dynamic_slice_in_dim(flat[: len(sums)], own * me, own, 1)
    mine_fc = lax.dynamic_slice_in_dim(flat[len(sums) :].reshape(-1), own_hidden * me, own_hidden)
    return (
        result.reshape(seq_count, part, width),
        grad_in.reshape(seq_count, part, width),
        mine[0],
        mine[1],
        total_qkv,
        mine[2],
        mine[3],
        total_out,
        mine[4],
        mine[5],
        mine[6],
        total_fc,
        mine_fc,
        total_proj,
        mine[7],
    )


def solution(mesh):
    return jax.shard_map(
        local,
        mesh=mesh,
        in_specs=(
            P("rep", "shard", None),
            P("rep", None),
            P("shard"),
            P("shard"),
            P("shard", None),
            P("shard"),
            P("shard"),
            P("shard", None),
            P("shard"),
            P("shard"),
            P("shard"),
            P("shard", None),
            P("shard"),
            P("shard", None),
            P("shard"),
            P("rep", "shard", None),
        ),
        out_specs=(
            P("rep", "shard", None),
            P("rep", "shard", None),
            P("shard"),
            P("shard"),
            P("shard", "rep"),
            P("shard"),
            P("shard"),
            P("shard", "rep"),
            P("shard"),
            P("shard"),
            P("shard"),
            P("shard", "rep"),
            P("shard"),
            P("shard", "rep"),
            P("shard"),
        ),
        check_vma=False,
    )
```

```python
import functools
import math

import jax
import jax.numpy as jnp
from jax import lax
from jax.experimental import pallas as pl
from jax.experimental.pallas import tpu as pltpu
from jax.sharding import PartitionSpec as P


HD = 64
MAX_DOC = 512

EPSILON = 1e-05
GELU_SCALE = math.sqrt(2.0 / math.pi)
BF16 = jnp.bfloat16
F32 = jnp.float32
NEG = -1e30
PAIR = 2 * HD


def layer_norm(values, gain, shift):
    centre_val = jnp.mean(values, axis=-1, keepdims=True)
    centred = values - centre_val
    variance = jnp.mean(centred * centred, axis=-1, keepdims=True)
    inverse = lax.rsqrt(variance + EPSILON)
    normed = centred * inverse
    return (normed * gain + shift, normed, inverse)


def norm_back(upstream, normed, inverse, gain):
    scaled = upstream * gain
    return inverse * (
        scaled
        - jnp.mean(scaled, axis=-1, keepdims=True)
        - normed * jnp.mean(scaled * normed, axis=-1, keepdims=True)
    )


def gelu_both(inputs_pre):
    square = inputs_pre * inputs_pre
    tangent = jnp.tanh(GELU_SCALE * (inputs_pre + 0.044715 * square * inputs_pre))
    value = 0.5 * inputs_pre * (1.0 + tangent)
    slope = 0.5 * (1.0 + tangent) + 0.5 * inputs_pre * (1.0 - tangent * tangent) * GELU_SCALE * (
        1.0 + 3.0 * 0.044715 * square
    )
    return value, slope


def dot_nn(a, b):
    return lax.dot_general(a, b, (((1,), (0,)), ((), ())), preferred_element_type=F32)


def dot_nt(a, b):
    return lax.dot_general(a, b, (((1,), (1,)), ((), ())), preferred_element_type=F32)


def dot_tn(a, b):
    return lax.dot_general(a, b, (((0,), (0,)), ((), ())), preferred_element_type=F32)


def block_at(me, j, count):
    k = jnp.bitwise_xor(me, j)
    return jnp.bitwise_and(k, 1) * (count // 2) + jnp.right_shift(k, 1)


def window_of(i, rows):
    back = -(-MAX_DOC // rows)
    return max(0, i - back) * rows, (i + 1) * rows


def mask_of(seg_row, seg_col, i, rows):
    lo, hi = window_of(i, rows)
    first = i * rows
    query_pos = first + lax.broadcasted_iota(jnp.int32, (rows, hi - lo), 0)
    key_pos = lo + lax.broadcasted_iota(jnp.int32, (rows, hi - lo), 1)
    same = seg_col[first : first + rows, :] == seg_row[:, lo:hi]
    return (key_pos <= query_pos) & same


def fwd_kernel(scale, rows, me_ref, seg_row, seg_col, qkv_ref, out_ref, lse_ref, ks, vs):
    count, part, width = qkv_ref.shape
    third = width // 3
    me = me_ref[0]
    spots = [block_at(me, j, count) for j in range(count)]
    per = rows // part
    left = lax.broadcasted_iota(jnp.int32, (1, PAIR), 1) < HD
    for pair in range(third // PAIR):
        at = pair * PAIR
        for j in range(count):
            ks[j * part : (j + 1) * part, :] = qkv_ref[spots[j], :, third + at : third + at + PAIR]
            vs[j * part : (j + 1) * part, :] = qkv_ref[
                spots[j], :, 2 * third + at : 2 * third + at + PAIR
            ]
        for i in range(count // per):
            lo, hi = window_of(i, rows)
            mask = mask_of(seg_row, seg_col, i, rows)
            q = jnp.concatenate(
                [qkv_ref[spots[i * per + b], :, at : at + PAIR] for b in range(per)], axis=0
            )
            kk, vv = ks[lo:hi, :], vs[lo:hi, :]
            mixed, totals = [], []
            for side in (left, ~left):
                qm = jnp.where(side, q, jnp.zeros_like(q))
                s = jnp.where(mask, dot_nt(qm, kk) * scale, NEG)
                top = jnp.max(s, axis=-1, keepdims=True)
                e = jnp.exp(s - top)
                total = jnp.sum(e, axis=-1, keepdims=True)
                mixed.append(dot_nn((e * (1.0 / total)).astype(BF16), vv))
                totals.append(top + jnp.log(total))
            o = jnp.where(left, mixed[0], mixed[1]).astype(BF16)
            t = jnp.where(left, totals[0], totals[1])
            for b in range(per):
                out_ref[spots[i * per + b], :, at : at + PAIR] = o[b * part : (b + 1) * part, :]
                lse_ref[spots[i * per + b], :, at : at + PAIR] = t[b * part : (b + 1) * part, :]


def bwd_kernel(
    scale, rows, me_ref, seg_row, seg_col, qkv_ref, grad_ref, lse_ref, out_ref, sum_ref, ks, vs, dk, dv
):
    count, part, width = qkv_ref.shape
    third = width // 3
    me = me_ref[0]
    spots = [block_at(me, j, count) for j in range(count)]
    per = rows // part
    left = lax.broadcasted_iota(jnp.int32, (1, PAIR), 1) < HD
    sum_ref[...] = jnp.zeros_like(sum_ref)
    for pair in range(third // PAIR):
        at = pair * PAIR
        for j in range(count):
            ks[j * part : (j + 1) * part, :] = qkv_ref[spots[j], :, third + at : third + at + PAIR]
            vs[j * part : (j + 1) * part, :] = qkv_ref[
                spots[j], :, 2 * third + at : 2 * third + at + PAIR
            ]
        dk[...] = jnp.zeros_like(dk)
        dv[...] = jnp.zeros_like(dv)
        q_sum = jnp.zeros((1, PAIR), F32)
        for i in range(count // per):
            lo, hi = window_of(i, rows)
            mask = mask_of(seg_row, seg_col, i, rows)
            here = [spots[i * per + b] for b in range(per)]
            q = jnp.concatenate([qkv_ref[h, :, at : at + PAIR] for h in here], axis=0)
            g = jnp.concatenate([grad_ref[h, :, at : at + PAIR] for h in here], axis=0)
            t = jnp.concatenate([lse_ref[h, :, at : at + PAIR] for h in here], axis=0)
            kk, vv = ks[lo:hi, :], vs[lo:hi, :]
            dq = None
            for number, side in enumerate((left, ~left)):
                qm = jnp.where(side, q, jnp.zeros_like(q))
                gm = jnp.where(side, g, jnp.zeros_like(g))
                km = jnp.where(side, kk, jnp.zeros_like(kk))
                lse = t[:, number * HD : number * HD + 1]
                probs = jnp.where(mask, jnp.exp(dot_nt(qm, kk) * scale - lse), 0.0)
                dp = dot_nt(gm, vv)
                delta = jnp.sum(probs * dp, axis=-1, keepdims=True)
                ds = (probs * (dp - delta) * scale).astype(BF16)
                part_q = dot_nn(ds, km)
                dq = part_q if dq is None else dq + part_q
                dk[lo:hi, :] += dot_tn(ds, qm)
                dv[lo:hi, :] += dot_tn(probs.astype(BF16), gm)
            q_sum = q_sum + jnp.sum(dq, axis=0, keepdims=True)
            dq = dq.astype(BF16)
            for b in range(per):
                out_ref[here[b], :, at : at + PAIR] = dq[b * part : (b + 1) * part, :]
        sum_ref[0:1, at : at + PAIR] = q_sum
        sum_ref[0:1, third + at : third + at + PAIR] = jnp.sum(dk[...], axis=0, keepdims=True)
        sum_ref[0:1, 2 * third + at : 2 * third + at + PAIR] = jnp.sum(
            dv[...], axis=0, keepdims=True
        )
        for j in range(count):
            out_ref[spots[j], :, third + at : third + at + PAIR] = dk[
                j * part : (j + 1) * part, :
            ].astype(BF16)
            out_ref[spots[j], :, 2 * third + at : 2 * third + at + PAIR] = dv[
                j * part : (j + 1) * part, :
            ].astype(BF16)


def attention_calls(count, part, slots, scale):
    length = count * part
    rows = 2 * part
    third = slots * HD
    vm = pl.BlockSpec(memory_space=pltpu.VMEM)
    sm = pl.BlockSpec(memory_space=pltpu.SMEM)
    fwd = pl.pallas_call(
        functools.partial(fwd_kernel, scale, rows),
        out_shape=(
            jax.ShapeDtypeStruct((count, part, third), BF16),
            jax.ShapeDtypeStruct((count, part, third), F32),
        ),
        in_specs=[sm, vm, vm, vm],
        out_specs=(vm, vm),
        scratch_shapes=[pltpu.VMEM((length, PAIR), BF16)] * 2,
        cost_estimate=pl.CostEstimate(
            flops=4 * length * length * third,
            bytes_accessed=length * third * 14,
            transcendentals=length * length * slots,
        ),
    )
    bwd = pl.pallas_call(
        functools.partial(bwd_kernel, scale, rows),
        out_shape=(
            jax.ShapeDtypeStruct((count, part, 3 * third), BF16),
            jax.ShapeDtypeStruct((8, 3 * third), F32),
        ),
        in_specs=[sm, vm, vm, vm, vm, vm],
        out_specs=(vm, vm),
        scratch_shapes=[pltpu.VMEM((length, PAIR), BF16)] * 2
        + [pltpu.VMEM((length, PAIR), F32)] * 2,
        cost_estimate=pl.CostEstimate(
            flops=10 * length * length * third,
            bytes_accessed=length * third * 18,
            transcendentals=length * length * slots,
        ),
    )
    return fwd, bwd


def pack_kernel(cuts, halves, base_ref, src_ref, out_ref):
    count, rows, width = out_ref.shape
    for d, runs in enumerate(cuts):
        place = jnp.bitwise_xor(base_ref[0], d)
        if halves:
            place = halves_order(place, len(cuts))

        @pl.when(place < count)
        def _(runs=runs, place=place):
            if sum(hi - lo for lo, hi, _ in runs) < width:
                out_ref[place] = jnp.zeros((rows, width), out_ref.dtype)
            for lo, hi, at in runs:
                out_ref[place, :, at : at + hi - lo] = src_ref[:, lo:hi]


def pack(src, base, halves, cuts, count, width):
    rows = src.shape[0]
    return pl.pallas_call(
        functools.partial(pack_kernel, cuts, halves),
        out_shape=jax.ShapeDtypeStruct((count, rows, width), src.dtype),
        in_specs=[pl.BlockSpec(memory_space=pltpu.SMEM), pl.BlockSpec(memory_space=pltpu.VMEM)],
        out_specs=pl.BlockSpec(memory_space=pltpu.VMEM),
        cost_estimate=pl.CostEstimate(
            flops=0, bytes_accessed=2 * src.size + 2 * count * rows * width, transcendentals=0
        ),
    )(base.astype(jnp.int32).reshape(1), src)


def share_kernel(plan, extra_at, share, room, me_ref, *refs):
    *sources, local_ref, tail_ref, out_ref, src_ref = refs
    place_blocks(me_ref[0], sources, src_ref)
    tail = out_ref.shape[2] - share - room
    extra = src_ref[0, :, extra_at:].astype(F32)
    for k in range(1, src_ref.shape[0]):
        extra = extra + src_ref[k, :, extra_at:].astype(F32)
    extra = (extra + local_ref[...]).astype(BF16)
    for q, runs in enumerate(plan):
        for d, lo, hi, at in runs:
            out_ref[q, :, at : at + hi - lo] = src_ref[d, :, lo:hi]
        out_ref[q, :, share : share + room] = extra[:, :room]
        out_ref[q, :, share + room :] = tail_ref[:, q * tail : (q + 1) * tail]


def to_shares(sources, me_word, local, tail, plan, extra_at, share, room):
    n = lax.axis_size("shard")
    rows, width = sources[0].shape[1:]
    each = share + room + tail.shape[1] // len(plan)
    vm = pl.BlockSpec(memory_space=pltpu.VMEM)
    return pl.pallas_call(
        functools.partial(share_kernel, plan, extra_at, share, room),
        out_shape=jax.ShapeDtypeStruct((len(plan), rows, each), BF16),
        in_specs=[pl.BlockSpec(memory_space=pltpu.SMEM), *source_specs(sources), vm, vm],
        out_specs=vm,
        scratch_shapes=[pltpu.VMEM((n, rows, width), BF16)],
        cost_estimate=pl.CostEstimate(
            flops=0, bytes_accessed=4 * n * rows * width, transcendentals=0
        ),
    )(me_word, *sources, local, tail)


def exchange(x, k):
    n = lax.axis_size("shard")
    return lax.ppermute(x, "shard", [(i, i ^ k) for i in range(n)])


def gather_halves(x):
    n = lax.axis_size("shard")
    others = [exchange(x, k) for k in range(2, n, 2)]
    near = jnp.concatenate([x] + others, axis=0)
    return near, exchange(near, 1)


def chip_sums(far, near):
    return near + exchange(far, 1).astype(F32)


def finish_sums(total, hold=None):
    n = lax.axis_size("shard")
    rows = total.shape[0] // (n // 2)
    out = total[:rows]
    for i, k in enumerate(range(2, n, 2)):
        send = total[(i + 1) * rows : (i + 2) * rows].astype(BF16)
        if hold is not None:
            send = after(send, hold)
        out = out + exchange(send, k).astype(F32)
    return out


def halves_order(k, n):
    return jnp.bitwise_and(k, 1) * (n // 2) + jnp.right_shift(k, 1)


def swap_packed(packed):
    n = lax.axis_size("shard")
    near = packed[: n // 2]
    got = exchange(packed[n // 2 :], 1)
    pairs = [
        exchange(jnp.stack([near[i], got[i]]), 2 * i) for i in range(1, n // 2)
    ]
    return (packed[:1], got[:1], *pairs)


def place_blocks(me, sources, dest_ref):
    for i, source in enumerate(sources):
        for k in range(1 if i < 2 else 2):
            there = jnp.bitwise_xor(me, i if i < 2 else 2 * i - 2 + k)
            dest_ref[there] = source[k]


def source_specs(sources):
    return [pl.BlockSpec(memory_space=pltpu.VMEM)] * len(sources)


def unpack_kernel(me_ref, *refs):
    place_blocks(me_ref[0], refs[:-1], refs[-1])


def unpack(sources):
    n = lax.axis_size("shard")
    shape = (n, *sources[0].shape[1:])
    size = math.prod(shape)
    return pl.pallas_call(
        unpack_kernel,
        out_shape=jax.ShapeDtypeStruct(shape, BF16),
        in_specs=[pl.BlockSpec(memory_space=pltpu.SMEM), *source_specs(sources)],
        out_specs=pl.BlockSpec(memory_space=pltpu.VMEM),
        cost_estimate=pl.CostEstimate(flops=0, bytes_accessed=4 * size, transcendentals=0),
    )(lax.axis_index("shard").astype(jnp.int32).reshape(1), *sources)


def pick(blocks, i):
    return lax.dynamic_index_in_dim(blocks, i, 0, keepdims=False)


def rep_scatter(blocks):
    return lax.psum_scatter(blocks, "rep", scatter_dimension=0).astype(F32)


def jointly(x, where):
    n, n_rep = lax.axis_size("shard"), lax.axis_size("rep")
    pairs = []
    for s in range(n):
        for r in range(n_rep):
            to_s, to_r = where(s, r)
            pairs.append((s * n_rep + r, to_s * n_rep + to_r))
    return lax.ppermute(x, ("shard", "rep"), pairs)


def by_parity(pair):
    even = jnp.bitwise_and(lax.axis_index("shard"), 1) == 0
    return jnp.where(even, pair[0], pair[1]), jnp.where(even, pair[1], pair[0])


def spread_columns(rows, own):
    n, n_rep = lax.axis_size("shard"), lax.axis_size("rep")
    cuts = [[(d * own, (d + 1) * own, 0)] for d in range(n)]
    if n != 2 * n_rep:
        packed = pack(rows, lax.axis_index("shard"), True, cuts, n, own)
        return unpack(swap_packed(packed)).reshape(-1, own)
    s, r = lax.axis_index("shard"), lax.axis_index("rep")
    mine = pack(rows, jnp.bitwise_xor(s, 2 * r), False, cuts, 2, own)
    pair = [
        jointly(mine[k], lambda i, j, k=k: (i ^ (2 * j + k), j)) for k in range(2)
    ]
    mine = jnp.stack(by_parity(pair))
    chip = jnp.right_shift(s, 1)
    everyone = lax.all_gather(mine, "rep", axis=0)
    return jnp.concatenate(
        [pick(everyone, jnp.bitwise_xor(chip, c)) for c in range(n_rep)], axis=0
    ).reshape(-1, own)


def to_halves(blocks):
    n = blocks.shape[0]
    me = lax.axis_index("shard")
    order = [*range(0, n, 2), *range(1, n, 2)]
    return jnp.stack([pick(blocks, jnp.bitwise_xor(me, k)) for k in order])


def collect_rows(part, own_rows, total_columns, hold=None):
    n, n_rep = lax.axis_size("shard"), lax.axis_size("rep")
    own = part.shape[1]
    if n == 2 * n_rep:
        summed = rep_scatter(part.reshape(n_rep, 2, own_rows, own)).astype(BF16)
        if hold is not None:
            summed = after(summed, hold)
        even = jnp.bitwise_and(lax.axis_index("shard"), 1) == 0
        pair = []
        for k in range(2):
            sent = jnp.where(even, summed[k], summed[1 - k])
            pair.append(jointly(sent, lambda i, j, k=k: (2 * j + ((i & 1) ^ k), i >> 1)))
        return jnp.concatenate(by_parity(pair), axis=1).astype(F32)
    swapped = unpack(swap_packed(to_halves(part.reshape(n, own_rows, own))))
    if n_rep <= n:
        swapped = swapped.reshape(n_rep, n // n_rep, own_rows, own)
        total = rep_scatter(swapped)
        return total.transpose(1, 0, 2).reshape(own_rows, total_columns // n_rep)
    swapped = swapped.reshape(n, own_rows, n_rep // n, total_columns // n_rep)
    return rep_scatter(swapped.transpose(0, 2, 1, 3).reshape(n_rep, own_rows, -1))


def after(value, *others):
    return lax.optimization_barrier((value,) + others)[0]


def local(
    tokens,
    segment_ids,
    ln1_gain,
    ln1_bias,
    w_qkv,
    q_bias,
    v_bias,
    w_out,
    out_bias,
    ln2_gain,
    ln2_bias,
    w_fc,
    fc_bias,
    w_proj,
    proj_bias,
    grad_out,
):
    seq_count, part, width = tokens.shape
    length = segment_ids.shape[1]
    n = lax.axis_size("shard")
    n_rep = lax.axis_size("rep")
    me = lax.axis_index("shard")
    own = ln1_gain.shape[0]
    own_hidden = fc_bias.shape[0]
    hidden_width = w_fc.shape[1]
    scale = float(HD) ** (-0.5)

    first_head = [-(-own * d // HD) for d in range(n + 1)]
    n_heads = [first_head[d + 1] - first_head[d] for d in range(n)]
    slots = 2 * -(-max(n_heads) // 2)
    third = slots * HD
    spill = max(HD * first_head[d] - own * d for d in range(n))
    head_of = lambda d: (own * d + HD - 1) // HD
    head_at = HD * head_of(me)
    head_shift = head_at - own * me
    head_rows = HD * head_of(me + 1) - head_at

    x_own = tokens.reshape(part, width)
    x_near, x_far = gather_halves(x_own)
    runs = [
        [
            (c * width + HD * first_head[d], c * width + HD * first_head[d + 1], c * third)
            for c in range(3)
        ]
        for d in range(n)
    ]
    pieces = pack(w_qkv, me, True, runs, n, 3 * third)
    qkv_w = unpack(swap_packed(pieces)).reshape(width, 3 * third)

    vectors = (ln1_gain, ln1_bias, q_bias, v_bias, out_bias, ln2_gain, ln2_bias, proj_bias)
    lanes = 128 * -(-own // 128)
    packed = jnp.pad(jnp.stack(vectors), ((0, 0), (0, lanes - own)))
    packed = after(packed, pieces)
    packed_near, packed_far = gather_halves(packed[None])
    packed_all = jnp.concatenate([packed_near, packed_far], axis=0)
    everyone = jnp.stack([pick(packed_all, block_at(me, d, n)) for d in range(n)])
    gain_one, shift_one, bias_q, bias_v, bias_out, gain_two, shift_two, bias_proj = [
        everyone[:, i, :own].reshape(width).astype(F32) for i in range(len(vectors))
    ]
    live = jnp.arange(third) < head_rows
    own_heads = lambda v: jnp.where(
        live, lax.dynamic_slice_in_dim(jnp.pad(v, (0, third)), head_at, third, 0), 0.0
    )
    bias_heads = jnp.concatenate([own_heads(bias_q), jnp.zeros(third, F32), own_heads(bias_v)])

    def first_half(x):
        ln_b = layer_norm(x.astype(F32), gain_one, shift_one)[0].astype(BF16)
        return ln_b, (dot_nn(ln_b, qkv_w) + bias_heads).astype(BF16)

    ln_one_near, qkv_near = first_half(x_near)
    ln_one_far, qkv_far = first_half(x_far)
    qkv = jnp.concatenate([qkv_near, qkv_far], axis=0).reshape(n, part, 3 * third)

    fc_w = spread_columns(after(w_fc, x_near), own_hidden)
    g_own = grad_out.reshape(part, width)
    g_near, g_far = gather_halves(after(g_own, qkv_w))
    out_next = lax.ppermute(after(w_out, qkv_w)[:spill], "shard", [(i, i - 1) for i in range(1, n)])
    out_ext = jnp.concatenate([w_out, out_next, jnp.zeros((third, width), BF16)], axis=0)
    out_w = jnp.where(
        live[:, None], lax.dynamic_slice_in_dim(out_ext, head_shift, third, 0), 0.0
    ).astype(BF16)

    seg_row = segment_ids.reshape(1, length)
    seg_col = segment_ids.reshape(length, 1)
    me_word = me.astype(jnp.int32).reshape(1)
    attend, attend_back = attention_calls(n, part, slots, scale)
    attended, lse = attend(me_word, seg_row, seg_col, qkv)
    attended = attended.reshape(length, third)
    half = length // 2
    attn_own = finish_sums(
        chip_sums(dot_nn(attended[half:], out_w).astype(BF16), dot_nn(attended[:half], out_w))
    )
    resid_in = x_own.astype(F32)
    mid = resid_in + attn_own + bias_out

    ln_two, normed_two, inverse_two = layer_norm(mid, gain_two, shift_two)
    ln_two_near, ln_two_far = gather_halves(ln_two.astype(BF16))
    bias_fc = fc_bias.astype(F32)

    def middle(ln_b, g):
        pre = dot_nn(ln_b, fc_w) + bias_fc
        value, slope = gelu_both(pre)
        grad_pre = dot_nt(g, w_proj) * slope
        return value.astype(BF16), grad_pre.astype(BF16), jnp.sum(grad_pre, axis=0)

    hidden_near, grad_pre_near, sum_near = middle(ln_two_near, g_near)
    hidden_far, grad_pre_far, sum_far = middle(ln_two_far, g_far)
    grad_partial_far = dot_nt(grad_pre_far, fc_w).astype(BF16)
    two_total = chip_sums(grad_partial_far, dot_nt(grad_pre_near, fc_w))
    grad_ln_two = finish_sums(two_total)
    late = two_total
    part_proj = dot_tn(after(hidden_near, late), g_near)
    part_proj = (part_proj + dot_tn(after(hidden_far, late), g_far)).astype(BF16)
    part_proj = part_proj.reshape(own_hidden, n_rep, width // n_rep).transpose(1, 0, 2)
    total_proj = rep_scatter(part_proj)
    part_fc = dot_tn(after(ln_two_near, late), grad_pre_near)
    part_fc = (part_fc + dot_tn(after(ln_two_far, late), grad_pre_far)).astype(BF16)

    grad_mid = g_own.astype(F32) + norm_back(grad_ln_two, normed_two, inverse_two, gain_two)

    gm_near, gm_far = gather_halves(grad_mid.astype(BF16))
    out_far = dot_nn(after(hidden_far, late), w_proj).astype(BF16)
    out_near = dot_nn(after(hidden_near, late), w_proj)
    out_total = chip_sums(out_far, out_near)
    grad_att = jnp.concatenate(
        [dot_nt(gm_near, out_w).astype(BF16), dot_nt(gm_far, out_w).astype(BF16)], axis=0
    ).reshape(n, part, third)
    grad_qkv, head_sums = attend_back(me_word, seg_row, seg_col, qkv, grad_att, lse)
    grad_qkv = grad_qkv.reshape(length, 3 * third)
    grad_w = dot_tn(ln_one_near, grad_qkv[:half]) + dot_tn(ln_one_far, grad_qkv[half:])
    part_qkv = grad_w.astype(BF16)

    def spread(v):
        room = jnp.zeros(width + third, F32)
        return lax.dynamic_update_slice_in_dim(room, jnp.where(live, v, 0.0), head_at, 0)[:width]

    w_wide = qkv_w.astype(F32)
    shift_sum = jnp.sum(w_wide * head_sums[0], axis=1)
    gain_sum = (jnp.sum(w_wide * grad_w, axis=1) - shift_one * shift_sum) / gain_one
    grad_top = g_own.astype(F32)
    sums = [
        gain_sum,
        shift_sum,
        spread(head_sums[0, :third]),
        spread(head_sums[0, 2 * third :]),
        jnp.sum(grad_mid, axis=0),
        jnp.sum(grad_ln_two * normed_two, axis=0),
        jnp.sum(grad_ln_two, axis=0),
        jnp.sum(grad_top, axis=0),
    ]
    ratio = own_hidden // own
    room = 16 * -(-(len(sums) + ratio) // 16)
    columns = jnp.pad(jnp.stack(sums), ((0, 128 - len(sums)), (0, 0))).astype(BF16).T
    hidden_sum = (sum_near + sum_far).reshape(own, ratio)
    local_extra = jnp.pad(hidden_sum, ((0, 0), (len(sums), 128 - len(sums) - ratio)))
    outgoing = jnp.concatenate([part_qkv, columns], axis=1).reshape(n, own, -1)
    incoming = swap_packed(to_halves(outgoing))
    one_far = dot_nt(after(grad_qkv, outgoing)[half:], qkv_w).astype(BF16)
    one_near = dot_nt(after(grad_qkv, outgoing)[:half], qkv_w)
    attended_late = after(attended, outgoing)
    part_out = dot_tn(attended_late[:half], gm_near)
    part_out = (part_out + dot_tn(attended_late[half:], gm_far)).astype(BF16)
    shifted = lax.dynamic_update_slice_in_dim(
        jnp.zeros((own + spill + third, width), BF16), part_out, head_shift, 0
    )
    before = lax.ppermute(shifted[own : own + spill], "shard", [(i, i + 1) for i in range(n - 1)])
    own_out = shifted[:own] + jnp.pad(before, ((0, own - spill), (0, 0)))
    share = 3 * width // n_rep
    plan = []
    for q in range(n_rep):
        cols = []
        for c in range(3):
            for d in range(n):
                start = c * width + HD * first_head[d]
                lo = max(start, q * share)
                hi = min(start + HD * n_heads[d], (q + 1) * share)
                if lo < hi:
                    base = c * third - start
                    cols.append((d, base + lo, base + hi, lo - q * share))
        plan.append(cols)
    shares = to_shares(
        incoming, me_word, local_extra, own_out, plan, 3 * third, share, room
    )
    total = rep_scatter(shares)
    total_qkv = total[:, :share]
    smalls = total[:, share : share + room].T
    total_out = total[:, share + room :]
    total_fc = collect_rows(part_fc, own, hidden_width, total)
    grad_ln_one = finish_sums(chip_sums(one_far, one_near), shares)
    result = mid + bias_proj + finish_sums(out_total, shares)

    _, normed_one, inverse_one = layer_norm(resid_in, gain_one, shift_one)
    grad_in = grad_mid + norm_back(grad_ln_one, normed_one, inverse_one, gain_one)

    mine = [smalls[i] for i in range(len(sums))]
    mine_fc = total[:, share + len(sums) : share + len(sums) + ratio].reshape(own_hidden)
    return (
        result.reshape(seq_count, part, width),
        grad_in.reshape(seq_count, part, width),
        mine[0],
        mine[1],
        total_qkv,
        mine[2],
        mine[3],
        total_out,
        mine[4],
        mine[5],
        mine[6],
        total_fc,
        mine_fc,
        total_proj,
        mine[7],
    )


def solution(mesh):
    return jax.shard_map(
        local,
        mesh=mesh,
        in_specs=(
            P("rep", "shard", None),
            P("rep", None),
            P("shard"),
            P("shard"),
            P("shard", None),
            P("shard"),
            P("shard"),
            P("shard", None),
            P("shard"),
            P("shard"),
            P("shard"),
            P("shard", None),
            P("shard"),
            P("shard", None),
            P("shard"),
            P("rep", "shard", None),
        ),
        out_specs=(
            P("rep", "shard", None),
            P("rep", "shard", None),
            P("shard"),
            P("shard"),
            P("shard", "rep"),
            P("shard"),
            P("shard"),
            P("shard", "rep"),
            P("shard"),
            P("shard"),
            P("shard"),
            P("shard", "rep"),
            P("shard"),
            P("shard", "rep"),
            P("shard"),
        ),
        check_vma=False,
    )
```

```python
import functools
import math

import jax
import jax.numpy as jnp
from jax import lax
from jax.experimental import pallas as pl
from jax.experimental.pallas import tpu as pltpu
from jax.sharding import PartitionSpec as P


HD = 64
MAX_DOC = 512

EPSILON = 1e-05
GELU_SCALE = math.sqrt(2.0 / math.pi)
BF16 = jnp.bfloat16
F32 = jnp.float32
NEG = -1e30
PAIR = 2 * HD


def layer_norm(values, gain, shift):
    centre_val = jnp.mean(values, axis=-1, keepdims=True)
    centred = values - centre_val
    variance = jnp.mean(centred * centred, axis=-1, keepdims=True)
    inverse = lax.rsqrt(variance + EPSILON)
    normed = centred * inverse
    return (normed * gain + shift, normed, inverse)


def norm_back(upstream, normed, inverse, gain):
    scaled = upstream * gain
    return inverse * (
        scaled
        - jnp.mean(scaled, axis=-1, keepdims=True)
        - normed * jnp.mean(scaled * normed, axis=-1, keepdims=True)
    )


def gelu_both(inputs_pre):
    square = inputs_pre * inputs_pre
    tangent = jnp.tanh(GELU_SCALE * (inputs_pre + 0.044715 * square * inputs_pre))
    value = 0.5 * inputs_pre * (1.0 + tangent)
    slope = 0.5 * (1.0 + tangent) + 0.5 * inputs_pre * (1.0 - tangent * tangent) * GELU_SCALE * (
        1.0 + 3.0 * 0.044715 * square
    )
    return value, slope


def dot_nn(a, b):
    return lax.dot_general(a, b, (((1,), (0,)), ((), ())), preferred_element_type=F32)


def dot_nt(a, b):
    return lax.dot_general(a, b, (((1,), (1,)), ((), ())), preferred_element_type=F32)


def dot_tn(a, b):
    return lax.dot_general(a, b, (((0,), (0,)), ((), ())), preferred_element_type=F32)


def block_at(me, j, count):
    k = jnp.bitwise_xor(me, j)
    return jnp.bitwise_and(k, 1) * (count // 2) + jnp.right_shift(k, 1)


def window_of(i, rows):
    back = -(-MAX_DOC // rows)
    return max(0, i - back) * rows, (i + 1) * rows


def mask_of(seg_row, seg_col, i, rows):
    lo, hi = window_of(i, rows)
    first = i * rows
    query_pos = first + lax.broadcasted_iota(jnp.int32, (rows, hi - lo), 0)
    key_pos = lo + lax.broadcasted_iota(jnp.int32, (rows, hi - lo), 1)
    same = seg_col[first : first + rows, :] == seg_row[:, lo:hi]
    return (key_pos <= query_pos) & same


def fwd_kernel(scale, rows, me_ref, seg_row, seg_col, qkv_ref, out_ref, lse_ref, ks, vs):
    count, part, width = qkv_ref.shape
    third = width // 3
    me = me_ref[0]
    spots = [block_at(me, j, count) for j in range(count)]
    per = rows // part
    left = lax.broadcasted_iota(jnp.int32, (1, PAIR), 1) < HD
    for pair in range(third // PAIR):
        at = pair * PAIR
        for j in range(count):
            ks[j * part : (j + 1) * part, :] = qkv_ref[spots[j], :, third + at : third + at + PAIR]
            vs[j * part : (j + 1) * part, :] = qkv_ref[
                spots[j], :, 2 * third + at : 2 * third + at + PAIR
            ]
        for i in range(count // per):
            lo, hi = window_of(i, rows)
            mask = mask_of(seg_row, seg_col, i, rows)
            q = jnp.concatenate(
                [qkv_ref[spots[i * per + b], :, at : at + PAIR] for b in range(per)], axis=0
            )
            kk, vv = ks[lo:hi, :], vs[lo:hi, :]
            mixed, totals = [], []
            for side in (left, ~left):
                qm = jnp.where(side, q, jnp.zeros_like(q))
                s = jnp.where(mask, dot_nt(qm, kk) * scale, NEG)
                top = jnp.max(s, axis=-1, keepdims=True)
                e = jnp.exp(s - top)
                total = jnp.sum(e, axis=-1, keepdims=True)
                mixed.append(dot_nn((e * (1.0 / total)).astype(BF16), vv))
                totals.append(top + jnp.log(total))
            o = jnp.where(left, mixed[0], mixed[1]).astype(BF16)
            t = jnp.where(left, totals[0], totals[1])
            for b in range(per):
                out_ref[spots[i * per + b], :, at : at + PAIR] = o[b * part : (b + 1) * part, :]
                lse_ref[spots[i * per + b], :, at : at + PAIR] = t[b * part : (b + 1) * part, :]


def bwd_kernel(
    scale, rows, me_ref, seg_row, seg_col, qkv_ref, grad_ref, lse_ref, out_ref, sum_ref, ks, vs, dk, dv
):
    count, part, width = qkv_ref.shape
    third = width // 3
    me = me_ref[0]
    spots = [block_at(me, j, count) for j in range(count)]
    per = rows // part
    left = lax.broadcasted_iota(jnp.int32, (1, PAIR), 1) < HD
    sum_ref[...] = jnp.zeros_like(sum_ref)
    for pair in range(third // PAIR):
        at = pair * PAIR
        for j in range(count):
            ks[j * part : (j + 1) * part, :] = qkv_ref[spots[j], :, third + at : third + at + PAIR]
            vs[j * part : (j + 1) * part, :] = qkv_ref[
                spots[j], :, 2 * third + at : 2 * third + at + PAIR
            ]
        dk[...] = jnp.zeros_like(dk)
        dv[...] = jnp.zeros_like(dv)
        q_sum = jnp.zeros((1, PAIR), F32)
        for i in range(count // per):
            lo, hi = window_of(i, rows)
            mask = mask_of(seg_row, seg_col, i, rows)
            here = [spots[i * per + b] for b in range(per)]
            q = jnp.concatenate([qkv_ref[h, :, at : at + PAIR] for h in here], axis=0)
            g = jnp.concatenate([grad_ref[h, :, at : at + PAIR] for h in here], axis=0)
            t = jnp.concatenate([lse_ref[h, :, at : at + PAIR] for h in here], axis=0)
            kk, vv = ks[lo:hi, :], vs[lo:hi, :]
            dq = None
            for number, side in enumerate((left, ~left)):
                qm = jnp.where(side, q, jnp.zeros_like(q))
                gm = jnp.where(side, g, jnp.zeros_like(g))
                km = jnp.where(side, kk, jnp.zeros_like(kk))
                lse = t[:, number * HD : number * HD + 1]
                probs = jnp.where(mask, jnp.exp(dot_nt(qm, kk) * scale - lse), 0.0)
                dp = dot_nt(gm, vv)
                delta = jnp.sum(probs * dp, axis=-1, keepdims=True)
                ds = (probs * (dp - delta) * scale).astype(BF16)
                part_q = dot_nn(ds, km)
                dq = part_q if dq is None else dq + part_q
                dk[lo:hi, :] += dot_tn(ds, qm)
                dv[lo:hi, :] += dot_tn(probs.astype(BF16), gm)
            q_sum = q_sum + jnp.sum(dq, axis=0, keepdims=True)
            dq = dq.astype(BF16)
            for b in range(per):
                out_ref[here[b], :, at : at + PAIR] = dq[b * part : (b + 1) * part, :]
        sum_ref[0:1, at : at + PAIR] = q_sum
        sum_ref[0:1, third + at : third + at + PAIR] = jnp.sum(dk[...], axis=0, keepdims=True)
        sum_ref[0:1, 2 * third + at : 2 * third + at + PAIR] = jnp.sum(
            dv[...], axis=0, keepdims=True
        )
        for j in range(count):
            out_ref[spots[j], :, third + at : third + at + PAIR] = dk[
                j * part : (j + 1) * part, :
            ].astype(BF16)
            out_ref[spots[j], :, 2 * third + at : 2 * third + at + PAIR] = dv[
                j * part : (j + 1) * part, :
            ].astype(BF16)


def attention_calls(count, part, slots, scale):
    length = count * part
    rows = 2 * part
    third = slots * HD
    vm = pl.BlockSpec(memory_space=pltpu.VMEM)
    sm = pl.BlockSpec(memory_space=pltpu.SMEM)
    fwd = pl.pallas_call(
        functools.partial(fwd_kernel, scale, rows),
        out_shape=(
            jax.ShapeDtypeStruct((count, part, third), BF16),
            jax.ShapeDtypeStruct((count, part, third), F32),
        ),
        in_specs=[sm, vm, vm, vm],
        out_specs=(vm, vm),
        scratch_shapes=[pltpu.VMEM((length, PAIR), BF16)] * 2,
        cost_estimate=pl.CostEstimate(
            flops=4 * length * length * third,
            bytes_accessed=length * third * 14,
            transcendentals=length * length * slots,
        ),
    )
    bwd = pl.pallas_call(
        functools.partial(bwd_kernel, scale, rows),
        out_shape=(
            jax.ShapeDtypeStruct((count, part, 3 * third), BF16),
            jax.ShapeDtypeStruct((8, 3 * third), F32),
        ),
        in_specs=[sm, vm, vm, vm, vm, vm],
        out_specs=(vm, vm),
        scratch_shapes=[pltpu.VMEM((length, PAIR), BF16)] * 2
        + [pltpu.VMEM((length, PAIR), F32)] * 2,
        cost_estimate=pl.CostEstimate(
            flops=10 * length * length * third,
            bytes_accessed=length * third * 18,
            transcendentals=length * length * slots,
        ),
    )
    return fwd, bwd


def pack_kernel(cuts, halves, base_ref, src_ref, out_ref):
    count, rows, width = out_ref.shape
    for d, runs in enumerate(cuts):
        place = jnp.bitwise_xor(base_ref[0], d)
        if halves:
            place = halves_order(place, len(cuts))

        @pl.when(place < count)
        def _(runs=runs, place=place):
            if sum(hi - lo for lo, hi, _ in runs) < width:
                out_ref[place] = jnp.zeros((rows, width), out_ref.dtype)
            for lo, hi, at in runs:
                out_ref[place, :, at : at + hi - lo] = src_ref[:, lo:hi]


def pack(src, base, halves, cuts, count, width):
    rows = src.shape[0]
    return pl.pallas_call(
        functools.partial(pack_kernel, cuts, halves),
        out_shape=jax.ShapeDtypeStruct((count, rows, width), src.dtype),
        in_specs=[pl.BlockSpec(memory_space=pltpu.SMEM), pl.BlockSpec(memory_space=pltpu.VMEM)],
        out_specs=pl.BlockSpec(memory_space=pltpu.VMEM),
        cost_estimate=pl.CostEstimate(
            flops=0, bytes_accessed=2 * src.size + 2 * count * rows * width, transcendentals=0
        ),
    )(base.astype(jnp.int32).reshape(1), src)


def share_kernel(plan, extra_at, share, room, me_ref, *refs):
    *sources, local_ref, tail_ref, out_ref, src_ref = refs
    place_blocks(me_ref[0], sources, src_ref)
    tail = out_ref.shape[2] - share - room
    extra = src_ref[0, :, extra_at:].astype(F32)
    for k in range(1, src_ref.shape[0]):
        extra = extra + src_ref[k, :, extra_at:].astype(F32)
    extra = (extra + local_ref[...]).astype(BF16)
    for q, runs in enumerate(plan):
        for d, lo, hi, at in runs:
            out_ref[q, :, at : at + hi - lo] = src_ref[d, :, lo:hi]
        out_ref[q, :, share : share + room] = extra[:, :room]
        out_ref[q, :, share + room :] = tail_ref[:, q * tail : (q + 1) * tail]


def to_shares(sources, me_word, local, tail, plan, extra_at, share, room):
    n = lax.axis_size("shard")
    rows, width = sources[0].shape[1:]
    each = share + room + tail.shape[1] // len(plan)
    vm = pl.BlockSpec(memory_space=pltpu.VMEM)
    return pl.pallas_call(
        functools.partial(share_kernel, plan, extra_at, share, room),
        out_shape=jax.ShapeDtypeStruct((len(plan), rows, each), BF16),
        in_specs=[pl.BlockSpec(memory_space=pltpu.SMEM), *source_specs(sources), vm, vm],
        out_specs=vm,
        scratch_shapes=[pltpu.VMEM((n, rows, width), BF16)],
        cost_estimate=pl.CostEstimate(
            flops=0, bytes_accessed=4 * n * rows * width, transcendentals=0
        ),
    )(me_word, *sources, local, tail)


def exchange(x, k):
    n = lax.axis_size("shard")
    return lax.ppermute(x, "shard", [(i, i ^ k) for i in range(n)])


def gather_halves(x):
    n = lax.axis_size("shard")
    others = [exchange(x, k) for k in range(2, n, 2)]
    near = jnp.concatenate([x] + others, axis=0)
    return near, exchange(near, 1)


def chip_sums(far, near):
    return near + exchange(far, 1).astype(F32)


def finish_sums(total, hold=None):
    n = lax.axis_size("shard")
    rows = total.shape[0] // (n // 2)
    out = total[:rows]
    for i, k in enumerate(range(2, n, 2)):
        send = total[(i + 1) * rows : (i + 2) * rows].astype(BF16)
        if hold is not None:
            send = after(send, hold)
        out = out + exchange(send, k).astype(F32)
    return out


def halves_order(k, n):
    return jnp.bitwise_and(k, 1) * (n // 2) + jnp.right_shift(k, 1)


def swap_packed(packed):
    n = lax.axis_size("shard")
    near = packed[: n // 2]
    got = exchange(packed[n // 2 :], 1)
    pairs = [
        exchange(jnp.stack([near[i], got[i]]), 2 * i) for i in range(1, n // 2)
    ]
    return (packed[:1], got[:1], *pairs)


def place_blocks(me, sources, dest_ref):
    for i, source in enumerate(sources):
        for k in range(1 if i < 2 else 2):
            there = jnp.bitwise_xor(me, i if i < 2 else 2 * i - 2 + k)
            dest_ref[there] = source[k]


def source_specs(sources):
    return [pl.BlockSpec(memory_space=pltpu.VMEM)] * len(sources)


def unpack_kernel(me_ref, *refs):
    place_blocks(me_ref[0], refs[:-1], refs[-1])


def unpack(sources):
    n = lax.axis_size("shard")
    shape = (n, *sources[0].shape[1:])
    size = math.prod(shape)
    return pl.pallas_call(
        unpack_kernel,
        out_shape=jax.ShapeDtypeStruct(shape, BF16),
        in_specs=[pl.BlockSpec(memory_space=pltpu.SMEM), *source_specs(sources)],
        out_specs=pl.BlockSpec(memory_space=pltpu.VMEM),
        cost_estimate=pl.CostEstimate(flops=0, bytes_accessed=4 * size, transcendentals=0),
    )(lax.axis_index("shard").astype(jnp.int32).reshape(1), *sources)


def pick(blocks, i):
    return lax.dynamic_index_in_dim(blocks, i, 0, keepdims=False)


def rep_scatter(blocks):
    return lax.psum_scatter(blocks, "rep", scatter_dimension=0).astype(F32)


def jointly(x, where):
    n, n_rep = lax.axis_size("shard"), lax.axis_size("rep")
    pairs = []
    for s in range(n):
        for r in range(n_rep):
            to_s, to_r = where(s, r)
            pairs.append((s * n_rep + r, to_s * n_rep + to_r))
    return lax.ppermute(x, ("shard", "rep"), pairs)


def by_parity(pair):
    even = jnp.bitwise_and(lax.axis_index("shard"), 1) == 0
    return jnp.where(even, pair[0], pair[1]), jnp.where(even, pair[1], pair[0])


def spread_columns(rows, own):
    n, n_rep = lax.axis_size("shard"), lax.axis_size("rep")
    cuts = [[(d * own, (d + 1) * own, 0)] for d in range(n)]
    if n != 2 * n_rep:
        packed = pack(rows, lax.axis_index("shard"), True, cuts, n, own)
        return unpack(swap_packed(packed)).reshape(-1, own)
    s, r = lax.axis_index("shard"), lax.axis_index("rep")
    mine = pack(rows, jnp.bitwise_xor(s, 2 * r), False, cuts, 2, own)
    pair = [
        jointly(mine[k], lambda i, j, k=k: (i ^ (2 * j + k), j)) for k in range(2)
    ]
    mine = jnp.stack(by_parity(pair))
    chip = jnp.right_shift(s, 1)
    everyone = lax.all_gather(mine, "rep", axis=0)
    return jnp.concatenate(
        [pick(everyone, jnp.bitwise_xor(chip, c)) for c in range(n_rep)], axis=0
    ).reshape(-1, own)


def to_halves(blocks):
    n = blocks.shape[0]
    me = lax.axis_index("shard")
    order = [*range(0, n, 2), *range(1, n, 2)]
    return jnp.stack([pick(blocks, jnp.bitwise_xor(me, k)) for k in order])


def swap_direct(blocks):
    n = lax.axis_size("shard")
    me = lax.axis_index("shard")
    picked = [pick(blocks, jnp.bitwise_xor(me, k)) for k in range(n)]
    return [picked[0]] + [exchange(picked[k], k) for k in range(1, n)]


def place_singles_kernel(me_ref, *refs):
    for k, source in enumerate(refs[:-1]):
        refs[-1][jnp.bitwise_xor(me_ref[0], k)] = source[...]


def place_singles(sources):
    shape = (len(sources), *sources[0].shape)
    vm = pl.BlockSpec(memory_space=pltpu.VMEM)
    return pl.pallas_call(
        place_singles_kernel,
        out_shape=jax.ShapeDtypeStruct(shape, BF16),
        in_specs=[pl.BlockSpec(memory_space=pltpu.SMEM), *[vm] * len(sources)],
        out_specs=vm,
        cost_estimate=pl.CostEstimate(
            flops=0, bytes_accessed=4 * math.prod(shape), transcendentals=0
        ),
    )(lax.axis_index("shard").astype(jnp.int32).reshape(1), *sources)


def collect_rows(part, own_rows, total_columns):
    n, n_rep = lax.axis_size("shard"), lax.axis_size("rep")
    own = part.shape[1]
    sources = swap_direct(part.reshape(n, own_rows, own))
    swapped = place_singles(sources)
    if n_rep <= n:
        return swapped.reshape(n_rep, n // n_rep, own_rows, own)
    swapped = swapped.reshape(n, own_rows, n_rep // n, total_columns // n_rep)
    return swapped.transpose(0, 2, 1, 3).reshape(n_rep, 1, own_rows, -1)


def after(value, *others):
    return lax.optimization_barrier((value,) + others)[0]


def local(
    tokens,
    segment_ids,
    ln1_gain,
    ln1_bias,
    w_qkv,
    q_bias,
    v_bias,
    w_out,
    out_bias,
    ln2_gain,
    ln2_bias,
    w_fc,
    fc_bias,
    w_proj,
    proj_bias,
    grad_out,
):
    seq_count, part, width = tokens.shape
    length = segment_ids.shape[1]
    n = lax.axis_size("shard")
    n_rep = lax.axis_size("rep")
    me = lax.axis_index("shard")
    own = ln1_gain.shape[0]
    own_hidden = fc_bias.shape[0]
    hidden_width = w_fc.shape[1]
    scale = float(HD) ** (-0.5)

    first_head = [-(-own * d // HD) for d in range(n + 1)]
    n_heads = [first_head[d + 1] - first_head[d] for d in range(n)]
    slots = 2 * -(-max(n_heads) // 2)
    third = slots * HD
    spill = max(HD * first_head[d] - own * d for d in range(n))
    head_of = lambda d: (own * d + HD - 1) // HD
    head_at = HD * head_of(me)
    head_shift = head_at - own * me
    head_rows = HD * head_of(me + 1) - head_at

    x_own = tokens.reshape(part, width)
    x_near, x_far = gather_halves(x_own)
    runs = [
        [
            (c * width + HD * first_head[d], c * width + HD * first_head[d + 1], c * third)
            for c in range(3)
        ]
        for d in range(n)
    ]
    pieces = pack(w_qkv, me, True, runs, n, 3 * third)
    qkv_w = unpack(swap_packed(pieces)).reshape(width, 3 * third)

    vectors = (ln1_gain, ln1_bias, q_bias, v_bias, out_bias, ln2_gain, ln2_bias, proj_bias)
    lanes = 128 * -(-own // 128)
    packed = jnp.pad(jnp.stack(vectors), ((0, 0), (0, lanes - own)))
    packed = after(packed, pieces)
    packed_near, packed_far = gather_halves(packed[None])
    packed_all = jnp.concatenate([packed_near, packed_far], axis=0)
    everyone = jnp.stack([pick(packed_all, block_at(me, d, n)) for d in range(n)])
    gain_one, shift_one, bias_q, bias_v, bias_out, gain_two, shift_two, bias_proj = [
        everyone[:, i, :own].reshape(width).astype(F32) for i in range(len(vectors))
    ]
    live = jnp.arange(third) < head_rows
    own_heads = lambda v: jnp.where(
        live, lax.dynamic_slice_in_dim(jnp.pad(v, (0, third)), head_at, third, 0), 0.0
    )
    bias_heads = jnp.concatenate([own_heads(bias_q), jnp.zeros(third, F32), own_heads(bias_v)])

    def first_half(x):
        ln_b = layer_norm(x.astype(F32), gain_one, shift_one)[0].astype(BF16)
        return ln_b, (dot_nn(ln_b, qkv_w) + bias_heads).astype(BF16)

    ln_one_near, qkv_near = first_half(x_near)
    ln_one_far, qkv_far = first_half(x_far)
    qkv = jnp.concatenate([qkv_near, qkv_far], axis=0).reshape(n, part, 3 * third)

    fc_w = spread_columns(after(w_fc, x_near), own_hidden)
    g_own = grad_out.reshape(part, width)
    g_near, g_far = gather_halves(after(g_own, qkv_w))
    out_next = lax.ppermute(after(w_out, qkv_w)[:spill], "shard", [(i, i - 1) for i in range(1, n)])
    out_ext = jnp.concatenate([w_out, out_next, jnp.zeros((third, width), BF16)], axis=0)
    out_w = jnp.where(
        live[:, None], lax.dynamic_slice_in_dim(out_ext, head_shift, third, 0), 0.0
    ).astype(BF16)

    seg_row = segment_ids.reshape(1, length)
    seg_col = segment_ids.reshape(length, 1)
    me_word = me.astype(jnp.int32).reshape(1)
    attend, attend_back = attention_calls(n, part, slots, scale)
    attended, lse = attend(me_word, seg_row, seg_col, qkv)
    attended = attended.reshape(length, third)
    half = length // 2
    attn_own = finish_sums(
        chip_sums(dot_nn(attended[half:], out_w).astype(BF16), dot_nn(attended[:half], out_w))
    )
    resid_in = x_own.astype(F32)
    mid = resid_in + attn_own + bias_out

    ln_two, normed_two, inverse_two = layer_norm(mid, gain_two, shift_two)
    ln_two_near, ln_two_far = gather_halves(ln_two.astype(BF16))
    bias_fc = fc_bias.astype(F32)

    def middle(ln_b, g):
        pre = dot_nn(ln_b, fc_w) + bias_fc
        value, slope = gelu_both(pre)
        grad_pre = dot_nt(g, w_proj) * slope
        return value.astype(BF16), grad_pre.astype(BF16), jnp.sum(grad_pre, axis=0)

    hidden_near, grad_pre_near, sum_near = middle(ln_two_near, g_near)
    hidden_far, grad_pre_far, sum_far = middle(ln_two_far, g_far)
    grad_partial_far = dot_nt(grad_pre_far, fc_w).astype(BF16)
    two_total = chip_sums(grad_partial_far, dot_nt(grad_pre_near, fc_w))
    grad_ln_two = finish_sums(two_total)
    late = two_total
    part_proj = dot_tn(after(hidden_near, late), g_near)
    part_proj = (part_proj + dot_tn(after(hidden_far, late), g_far)).astype(BF16)
    part_proj = part_proj.reshape(own_hidden, n_rep, width // n_rep).transpose(1, 0, 2)
    total_proj = rep_scatter(part_proj)
    part_fc = dot_tn(after(ln_two_near, late), grad_pre_near)
    part_fc = (part_fc + dot_tn(after(ln_two_far, late), grad_pre_far)).astype(BF16)

    grad_mid = g_own.astype(F32) + norm_back(grad_ln_two, normed_two, inverse_two, gain_two)

    gm_near, gm_far = gather_halves(grad_mid.astype(BF16))
    out_far = dot_nn(after(hidden_far, late), w_proj).astype(BF16)
    out_near = dot_nn(after(hidden_near, late), w_proj)
    out_total = chip_sums(out_far, out_near)
    shares_fc = collect_rows(after(part_fc, gm_near), own, hidden_width)
    total_fc = rep_scatter(shares_fc)
    total_fc = total_fc.transpose(1, 0, 2).reshape(own, hidden_width // n_rep)
    grad_att = jnp.concatenate(
        [dot_nt(gm_near, out_w).astype(BF16), dot_nt(gm_far, out_w).astype(BF16)], axis=0
    ).reshape(n, part, third)
    grad_qkv, head_sums = attend_back(me_word, seg_row, seg_col, qkv, grad_att, lse)
    grad_qkv = grad_qkv.reshape(length, 3 * third)
    grad_w = dot_tn(ln_one_near, grad_qkv[:half]) + dot_tn(ln_one_far, grad_qkv[half:])
    part_qkv = after(grad_w.astype(BF16), shares_fc)

    def spread(v):
        room = jnp.zeros(width + third, F32)
        return lax.dynamic_update_slice_in_dim(room, jnp.where(live, v, 0.0), head_at, 0)[:width]

    w_wide = qkv_w.astype(F32)
    shift_sum = jnp.sum(w_wide * head_sums[0], axis=1)
    gain_sum = (jnp.sum(w_wide * grad_w, axis=1) - shift_one * shift_sum) / gain_one
    grad_top = g_own.astype(F32)
    sums = [
        gain_sum,
        shift_sum,
        spread(head_sums[0, :third]),
        spread(head_sums[0, 2 * third :]),
        jnp.sum(grad_mid, axis=0),
        jnp.sum(grad_ln_two * normed_two, axis=0),
        jnp.sum(grad_ln_two, axis=0),
        jnp.sum(grad_top, axis=0),
    ]
    ratio = own_hidden // own
    room = 16 * -(-(len(sums) + ratio) // 16)
    columns = jnp.pad(jnp.stack(sums), ((0, 128 - len(sums)), (0, 0))).astype(BF16).T
    outgoing = jnp.concatenate([part_qkv, columns], axis=1).reshape(n, own, -1)
    incoming = swap_packed(to_halves(outgoing))
    hidden_sum = after(sum_near + sum_far, outgoing).reshape(own, ratio)
    local_extra = jnp.pad(hidden_sum, ((0, 0), (len(sums), 128 - len(sums) - ratio)))
    one_far = dot_nt(after(grad_qkv, outgoing)[half:], qkv_w).astype(BF16)
    one_near = dot_nt(after(grad_qkv, outgoing)[:half], qkv_w)
    attended_late = after(attended, outgoing)
    part_out = dot_tn(attended_late[:half], gm_near)
    part_out = (part_out + dot_tn(attended_late[half:], gm_far)).astype(BF16)
    shifted = lax.dynamic_update_slice_in_dim(
        jnp.zeros((own + spill + third, width), BF16), part_out, head_shift, 0
    )
    before = lax.ppermute(shifted[own : own + spill], "shard", [(i, i + 1) for i in range(n - 1)])
    own_out = shifted[:own] + jnp.pad(before, ((0, own - spill), (0, 0)))
    share = 3 * width // n_rep
    plan = []
    for q in range(n_rep):
        cols = []
        for c in range(3):
            for d in range(n):
                start = c * width + HD * first_head[d]
                lo = max(start, q * share)
                hi = min(start + HD * n_heads[d], (q + 1) * share)
                if lo < hi:
                    base = c * third - start
                    cols.append((d, base + lo, base + hi, lo - q * share))
        plan.append(cols)
    shares = to_shares(
        incoming, me_word, local_extra, own_out, plan, 3 * third, share, room
    )
    total = rep_scatter(shares)
    total_qkv = total[:, :share]
    smalls = total[:, share : share + room].T
    total_out = total[:, share + room :]
    grad_ln_one = finish_sums(chip_sums(one_far, one_near), shares)
    result = mid + bias_proj + finish_sums(out_total, shares)

    _, normed_one, inverse_one = layer_norm(resid_in, gain_one, shift_one)
    grad_in = grad_mid + norm_back(grad_ln_one, normed_one, inverse_one, gain_one)

    mine = [smalls[i] for i in range(len(sums))]
    mine_fc = total[:, share + len(sums) : share + len(sums) + ratio].reshape(own_hidden)
    return (
        result.reshape(seq_count, part, width),
        grad_in.reshape(seq_count, part, width),
        mine[0],
        mine[1],
        total_qkv,
        mine[2],
        mine[3],
        total_out,
        mine[4],
        mine[5],
        mine[6],
        total_fc,
        mine_fc,
        total_proj,
        mine[7],
    )


def solution(mesh):
    return jax.shard_map(
        local,
        mesh=mesh,
        in_specs=(
            P("rep", "shard", None),
            P("rep", None),
            P("shard"),
            P("shard"),
            P("shard", None),
            P("shard"),
            P("shard"),
            P("shard", None),
            P("shard"),
            P("shard"),
            P("shard"),
            P("shard", None),
            P("shard"),
            P("shard", None),
            P("shard"),
            P("rep", "shard", None),
        ),
        out_specs=(
            P("rep", "shard", None),
            P("rep", "shard", None),
            P("shard"),
            P("shard"),
            P("shard", "rep"),
            P("shard"),
            P("shard"),
            P("shard", "rep"),
            P("shard"),
            P("shard"),
            P("shard"),
            P("shard", "rep"),
            P("shard"),
            P("shard", "rep"),
            P("shard"),
        ),
        check_vma=False,
    )
```
